32 devices in a mesh: row: 4 (over z), col: 8 (over y, x, core).
Axes of the slice: x: 2, y: 2, z: 4, core: 2. Of those that a mesh axis runs over, the one named last changes fastest.
Arguments:
- panel: float32 [8, 1024, 8192], P(None, 'row', 'col'), may hold values from -0.0625 to 0.0625
- prior_y: float32 [8192, 1024], P('col', 'row'), may hold values from -6 to 6
- right_side: float32 [8, 1024, 1024], P(None, 'row', 'col'), may hold values from -6 to 6
- inv_blocks: float32 [2, 1024, 1024], P(None, 'row'), may hold values from -2 to 2, as said below
- lower_block: float32 [1024, 1024], P('row'), may hold values from -0.1875 to 0.1875
Outputs:
- y_window: float32 [2, 1024, 1024], P(None, 'row', 'col')
- pending: float32 [6, 1024, 1024], P(None, 'row', 'col')
The draws below stay inside these ranges and needn't reach their ends.
Inputs may be any that keep to these rules, and one draw needn't show every extreme that they name: `inv_blocks`: each block is lower triangular with a positive diagonal.
All inputs are finite; a program needn't handle non-finite values.
Results may differ from the reference program's by a relative error of at most 0.000073.
Values sent between devices are 32-bit elements; how exact they have to be, the bound alone decides.
A program may use at most 64 MiB of HBM per device.

```python
import math
import jax
import jax.numpy as jnp
from jax import lax

BS = 1024
M = 1024
STEPS = 8
PRIOR = 8192


def draw_inv_blocks(key, part):
    key_diag, key_off = jax.random.split(key, 2)
    indices = jnp.arange(BS)
    strict = (indices[:, None] > indices[None, :]).astype(jnp.float32)
    identity = (indices[:, None] == indices[None, :]).astype(jnp.float32)
    diagonal = jnp.exp(jax.random.uniform(key_diag, (2, BS), jnp.float32, math.log(0.5), math.log(2.0)))
    offdiag = jax.random.normal(key_off, (2, BS, BS), jnp.float32) * (0.6 / math.sqrt(BS))
    offdiag = jnp.clip(offdiag, -1.5, 1.5)
    return offdiag * strict + identity * diagonal[:, :, None]


def raised(array, key, source, target, shards_of, factor):
    owner, partner = [(jnp.arange(array.shape[dim]) // (array.shape[dim] // shards_of)).reshape([-1 if axis == dim else 1 for axis in range(array.ndim)]) for dim in (source, target)]
    chosen = jax.random.permutation(key, shards_of)[partner]
    strong = (owner == chosen) | (owner == (partner + shards_of // 2) % shards_of)
    return jnp.where(strong, factor * array, array)


def shard_levels(own_key, extent, cuts, smallest, high):
    gain = 1.0
    for dim, parts in cuts:
        steps = jax.random.uniform(jax.random.fold_in(jax.random.fold_in(own_key, 6), dim), (parts,), jnp.float32, smallest / len(cuts), high / len(cuts))
        gain = gain * jnp.repeat(jnp.exp(steps), extent[dim] // parts).reshape((-1,) + (1,) * (len(extent) - 1 - dim))
    return gain


def gaussian(stream_key, shape, width, reach, shards=(), held_as=jnp.bfloat16):
    entries = width * jax.random.normal(stream_key, shape, jnp.float32)
    if shards:
        entries = entries * shard_levels(stream_key, shape, shards, -0.22, 0.18)
    return jnp.clip(entries, -reach, reach).astype(held_as)


def noise_with(own_key, shape, spread, limit, shards, heavy, held_as=jnp.bfloat16):
    drawn = spread * jax.random.normal(own_key, shape, jnp.float32)
    if shards:
        drawn = drawn * shard_levels(own_key, shape, shards, -0.22, 0.18)
    return jnp.clip(raised(drawn, jax.random.fold_in(own_key, 3), *heavy), -limit, limit).astype(held_as)


def setup_inputs(seed: int = 0) -> dict:
    key_of = jax.random.split(jax.random.key(seed), 6)
    panel = gaussian(key_of[0], (STEPS, BS, PRIOR), PRIOR ** -0.5, 0.0625, ((1, 4), (2, 8)), jnp.float32)
    prior_y = noise_with(key_of[1], (PRIOR, M), 1.0, 6.0, ((0, 8), (1, 4)), (0, 1, 8, 2.0), jnp.float32)
    right_side = gaussian(key_of[2], (STEPS, BS, M), 1.0, 6.0, ((1, 4), (2, 8)), jnp.float32)
    inv_blocks = draw_inv_blocks(jax.random.fold_in(key_of[5], 71), 0)
    lower_block = gaussian(key_of[4], (BS, BS), BS ** -0.5, 0.1875, ((0, 4),), jnp.float32)
    return dict(panel=panel, prior_y=prior_y, right_side=right_side, inv_blocks=inv_blocks, lower_block=lower_block)


def reference(panel, prior_y, right_side, inv_blocks, lower_block):
    highest = lax.Precision.HIGHEST
    panel_total = jnp.einsum("sip,pm->sim", panel, prior_y, precision=highest, preferred_element_type=jnp.float32)
    residual = right_side - panel_total
    first_solution = jnp.dot(inv_blocks[0], residual[0], precision=highest, preferred_element_type=jnp.float32)
    second_residual = residual[1] - jnp.dot(lower_block, first_solution, precision=highest, preferred_element_type=jnp.float32)
    second_solution = jnp.dot(inv_blocks[1], second_residual, precision=highest, preferred_element_type=jnp.float32)
    return (jnp.stack([first_solution, second_solution]), residual[2:])
```

```python
import functools

import jax
import jax.numpy as jnp
from jax import lax
from jax.experimental import pallas as pl
from jax.experimental.pallas import tpu as pltpu
from jax.sharding import PartitionSpec as P

MESH = pl.DeviceIdType.MESH
F32 = jnp.float32
BF16 = jnp.bfloat16


def split(x):
    high = x.astype(BF16)
    return high, (x - high.astype(F32)).astype(BF16)


def dot3(a, b):
    a_hi, a_lo = a
    b_hi, b_lo = b
    dot = functools.partial(jnp.dot, preferred_element_type=F32)
    return dot(a_hi, b_hi) + (dot(a_hi, b_lo) + dot(a_lo, b_hi))


def kernel(
    panel, prior, right, inv, lower, y_out, pend_out,
    pf, p_hi, p_lo, y_buf, y_hi, y_lo, core_src, core_dst, part, first_dst, second_dst,
    rhs, inv_v, low_v, r0_all, y0_all, s1_all, r1,
    load_sem, panel_sem, y_send, y_recv, core_send, core_recv, first_send, first_recv,
    second_send, second_recv, chain_send, chain_recv,
):
    steps, rows, depth = pf.shape
    chunks = core_send.shape[1]
    per = steps // chunks
    z = lax.axis_index("row")
    col = lax.axis_index("col")
    y, x, core = col // 4, (col // 2) % 2, col % 2
    chip = col // 2
    sibling = col + 1 - 2 * core
    x_near, y_near = col + 2 - 4 * x, col + 4 - 8 * y
    first = x_near + core * (y_near - x_near)
    second = y_near + core * (x_near - y_near)
    f = x + core * (y - x)
    g = y + core * (x - y)
    middle = (z == 1) | (z == 2)
    upper = z // 2
    z_fold = z + upper * (3 - 2 * z)

    def block_at(k):
        b = (z_fold, 1 - z_fold, 2, 3)[k]
        return b + upper * (3 - 2 * b)

    own = pltpu.make_async_copy(prior, y_buf.at[z], load_sem.at[0])
    own.start()
    panel_copies = [
        pltpu.make_async_copy(panel.at[s], pf.at[s], panel_sem.at[s]) for s in range(steps)
    ]
    for copy in panel_copies:
        copy.start()
    loads = [
        pltpu.make_async_copy(right, rhs, load_sem.at[1]),
        pltpu.make_async_copy(inv, inv_v, load_sem.at[2]),
        pltpu.make_async_copy(lower, low_v, load_sem.at[3]),
    ]
    for copy in loads:
        copy.start()

    barrier = pltpu.get_barrier_semaphore()
    for partner in (sibling, x_near, y_near):
        pl.semaphore_signal(barrier, inc=1, device_id=(z, partner), device_id_type=MESH)
    for j in range(1, 4):
        pl.semaphore_signal(barrier, inc=1, device_id=((z + j) % 4, col), device_id_type=MESH)
    pl.semaphore_wait(barrier, 6)

    def along_z(src, b, target, sem):
        return pltpu.make_async_remote_copy(
            src_ref=src, dst_ref=y_buf.at[b], send_sem=y_send.at[sem], recv_sem=y_recv.at[b],
            device_id=(target, col), device_id_type=MESH,
        )

    def forward(b, finish=False):
        @pl.when((b < z) & (z < 3))
        def _():
            copy = along_z(y_buf.at[b], b, z + 1, 2 + b)
            copy.wait_send() if finish else copy.start()

        @pl.when((b > z) & (z > 0))
        def _():
            copy = along_z(y_buf.at[b], b, z - 1, 2 + b)
            copy.wait_send() if finish else copy.start()

    def own_sends(finish=False):
        @pl.when(z < 3)
        def _():
            copy = along_z(prior, z, z + 1, 0)
            copy.wait_send() if finish else copy.start()

        @pl.when(z > 0)
        def _():
            copy = along_z(prior, z, z - 1, 1)
            copy.wait_send() if finish else copy.start()

    def arrived(b):
        along_z(y_buf.at[b], b, (z + 1) % 4, 0).wait_recv()

    def piece(ref, k, c):
        return ref.at[k, pl.ds(c * per, per)]

    def core_copy(k, c):
        return pltpu.make_async_remote_copy(
            src_ref=piece(core_src, k, c), dst_ref=piece(core_dst, k, c),
            send_sem=core_send.at[k, c], recv_sem=core_recv.at[k, c],
            device_id=(z, sibling), device_id_type=MESH,
        )

    def first_copy(k, c):
        return pltpu.make_async_remote_copy(
            src_ref=piece(part, k, c), dst_ref=piece(first_dst, k, c),
            send_sem=first_send.at[k, c], recv_sem=first_recv.at[k, c],
            device_id=(z, first), device_id_type=MESH,
        )

    def second_copy(k, c):
        return pltpu.make_async_remote_copy(
            src_ref=piece(part, k, c), dst_ref=second_dst.at[pl.ds(c * per, per)],
            send_sem=second_send.at[c], recv_sem=second_recv.at[c],
            device_id=(z, second), device_id_type=MESH,
        )

    def goal(k):
        b = block_at(k)
        y_b, x_b = b // 2, b % 2
        return x_b + core * (y_b - x_b), y_b + core * (x_b - y_b)

    def multiply(k):
        y_high, y_low = split(y_buf[block_at(k)])
        y_hi[...] = y_high
        y_lo[...] = y_low

        @pl.loop(0, steps)
        def _(s):
            if k == 0:
                pltpu.make_async_copy(panel.at[s], pf.at[s], panel_sem.at[s]).wait()
                high, low = split(pf[s])
                p_hi[s] = high
                p_lo[s] = low
            terms = dot3((p_hi[s], p_lo[s]), (y_hi[...], y_lo[...]))
            half = terms.shape[1] // 2
            part[k, s] = jnp.where(core == 0, terms[:, :half], terms[:, half:])
            core_src[k, s] = jnp.where(core == 0, terms[:, half:], terms[:, :half])

            @pl.when(s % per == per - 1)
            def _():
                core_copy(k, s // per).start()

    def add_core(k):
        f_b, _ = goal(k)

        @pl.loop(0, chunks)
        def _(c):
            core_copy(k, c).wait_recv()
            here = pl.ds(c * per, per)
            part[k, here] = part[k, here] + core_dst[k, here]

            @pl.when(f != f_b)
            def _():
                first_copy(k, c).start()

    def add_first(k):
        f_b, g_b = goal(k)

        @pl.when(f == f_b)
        def _():
            @pl.loop(0, chunks)
            def _(c):
                first_copy(k, c).wait_recv()
                here = pl.ds(c * per, per)
                part[k, here] = part[k, here] + first_dst[k, here]

                @pl.when(g != g_b)
                def _():
                    second_copy(k, c).start()

    def chain_copy(which, ref, target, source):
        here = ref.at[pl.ds(pl.multiple_of(source * rows, rows), rows)]
        return pltpu.make_async_remote_copy(
            src_ref=here, dst_ref=here, send_sem=chain_send.at[which, target],
            recv_sem=chain_recv.at[which, source],
            device_id=(target, col), device_id_type=MESH,
        )

    def spread(which, ref, down, finish=False):
        for target in range(4):
            @pl.when((z != target) if down else (z < target))
            def _():
                copy = chain_copy(which, ref, target, z)
                copy.wait_send() if finish else copy.start()

    def collect(which, ref, down):
        for source in range(4):
            @pl.when((z != source) if down else (z > source))
            def _():
                chain_copy(which, ref, (z + 1) % 4, source).wait_recv()

    mine = pl.ds(pl.multiple_of(z * rows, rows), rows)

    def finish_block(k):
        @pl.when(block_at(k) == chip)
        def _():
            for c in range(chunks):
                second_copy(k, c).wait_recv()
                for s in range(c * per, (c + 1) * per):
                    rest = rhs[s] - (part[k, s] + second_dst[s])
                    if s == 0:
                        r0_all[mine, :] = rest
                        spread(0, r0_all, False)
                    elif s == 1:
                        r1[...] = rest
                    else:
                        pend_out[s - 2] = rest

    own_sends()
    for ref in (r0_all, s1_all):
        for source in range(4):
            @pl.when(source > z)
            def _(ref=ref, source=source):
                ref[source * rows:(source + 1) * rows, :] = jnp.zeros((rows, ref.shape[1]), F32)
    own.wait()
    multiply(0)
    for copy in loads:
        copy.wait()
    add_core(0)

    for k in range(1, 4):
        if k == 2:
            @pl.when(jnp.logical_not(middle))
            def _():
                arrived(block_at(2))
        else:
            arrived(block_at(k))
            forward(block_at(k))
        if k == 1:
            @pl.when(middle)
            def _():
                arrived(block_at(2))
                forward(block_at(2))
        multiply(k)
        add_first(k - 1)
        add_core(k)
        finish_block(k - 1)
    add_first(3)
    finish_block(3)

    collect(0, r0_all, False)
    first_solution = dot3(split(inv_v[0]), split(r0_all[...]))
    y0_all[mine, :] = first_solution
    spread(1, y0_all, True)
    y_out[0] = first_solution
    collect(1, y0_all, True)
    s1_all[mine, :] = r1[...] - dot3(split(low_v[...]), split(y0_all[...]))
    spread(2, s1_all, False)
    collect(2, s1_all, False)
    y_out[1] = dot3(split(inv_v[1]), split(s1_all[...]))

    own_sends(True)
    for k in range(1, 4):
        forward(block_at(k), True)
    for k in range(4):
        f_b, g_b = goal(k)

        @pl.loop(0, chunks)
        def _(c):
            core_copy(k, c).wait_send()

            @pl.when(f != f_b)
            def _():
                first_copy(k, c).wait_send()

            @pl.when((f == f_b) & (g != g_b))
            def _():
                second_copy(k, c).wait_send()

    spread(0, r0_all, False, True)
    spread(1, y0_all, True, True)
    spread(2, s1_all, False, True)


def fused(panel, prior_y, right_side, inv_blocks, lower_block):
    steps, rows, depth = panel.shape
    wide = prior_y.shape[1]
    own = right_side.shape[2]
    size = inv_blocks.shape[2]
    chunks = 4
    anywhere = pl.BlockSpec(memory_space=pl.ANY)
    local = pl.BlockSpec(memory_space=pltpu.VMEM)
    dma = pltpu.SemaphoreType.DMA
    return pl.pallas_call(
        kernel,
        out_shape=(
            jax.ShapeDtypeStruct((2, rows, own), F32),
            jax.ShapeDtypeStruct((steps - 2, rows, own), F32),
        ),
        in_specs=[anywhere] * 5,
        out_specs=(local, local),
        scratch_shapes=[
            pltpu.VMEM((steps, rows, depth), F32),
            pltpu.VMEM((steps, rows, depth), BF16),
            pltpu.VMEM((steps, rows, depth), BF16),
            pltpu.VMEM((4, depth, wide), F32),
            pltpu.VMEM((depth, wide), BF16),
            pltpu.VMEM((depth, wide), BF16),
            pltpu.VMEM((4, steps, rows, own), F32),
            pltpu.VMEM((4, steps, rows, own), F32),
            pltpu.VMEM((4, steps, rows, own), F32),
            pltpu.VMEM((4, steps, rows, own), F32),
            pltpu.VMEM((steps, rows, own), F32),
            pltpu.VMEM((steps, rows, own), F32),
            pltpu.VMEM((2, rows, size), F32),
            pltpu.VMEM((rows, size), F32),
            pltpu.VMEM((size, own), F32),
            pltpu.VMEM((size, own), F32),
            pltpu.VMEM((size, own), F32),
            pltpu.VMEM((rows, own), F32),
            dma((4,)),
            dma((steps,)),
            dma((6,)),
            dma((4,)),
            dma((4, chunks)),
            dma((4, chunks)),
            dma((4, chunks)),
            dma((4, chunks)),
            dma((chunks,)),
            dma((chunks,)),
            dma((3, 4)),
            dma((3, 4)),
        ],
        compiler_params=pltpu.CompilerParams(
            collective_id=0, has_side_effects=True, vmem_limit_bytes=60 * 1024 * 1024
        ),
    )(panel, prior_y, right_side, inv_blocks, lower_block)


def general(panel, prior_y, right_side, inv_blocks, lower_block):
    highest = lax.Precision.HIGHEST
    terms = jnp.einsum(
        "sip,pm->sim",
        panel,
        lax.all_gather(prior_y, "row", axis=1, tiled=True),
        precision=highest,
        preferred_element_type=jnp.float32,
    )
    panel_total = lax.psum_scatter(terms, "col", scatter_dimension=2, tiled=True)
    residual = right_side - panel_total
    first_all_rows = lax.all_gather(residual[0], "row", axis=0, tiled=True)
    first_solution = jnp.dot(
        inv_blocks[0], first_all_rows, precision=highest, preferred_element_type=jnp.float32
    )
    solved_all = lax.all_gather(first_solution, "row", axis=0, tiled=True)
    second_residual = residual[1] - jnp.dot(
        lower_block, solved_all, precision=highest, preferred_element_type=jnp.float32
    )
    second_all_rows = lax.all_gather(second_residual, "row", axis=0, tiled=True)
    second_solution = jnp.dot(
        inv_blocks[1], second_all_rows, precision=highest, preferred_element_type=jnp.float32
    )
    return (jnp.stack([first_solution, second_solution]), residual[2:])


def solution(mesh):
    placed = (
        P(None, "row", "col"),
        P("col", "row"),
        P(None, "row", "col"),
        P(None, "row", None),
        P("row", None),
    )
    four_by_eight = mesh.shape["row"] == 4 and mesh.shape["col"] == 8
    return jax.shard_map(
        fused if four_by_eight else general,
        mesh=mesh,
        in_specs=placed,
        out_specs=(P(None, "row", "col"), P(None, "row", "col")),
        check_vma=False,
    )
```

```python
import functools

import jax
import jax.numpy as jnp
from jax import lax
from jax.experimental import pallas as pl
from jax.experimental.pallas import tpu as pltpu
from jax.sharding import PartitionSpec as P

MESH = pl.DeviceIdType.MESH
F32 = jnp.float32
BF16 = jnp.bfloat16


def split(x):
    high = x.astype(BF16)
    return high, (x - high.astype(F32)).astype(BF16)


def dot3(a, b):
    a_hi, a_lo = a
    b_hi, b_lo = b
    dot = functools.partial(jnp.dot, preferred_element_type=F32)
    return dot(a_hi, b_hi) + (dot(a_hi, b_lo) + dot(a_lo, b_hi))


def kernel(
    panel, prior, right, inv, lower, y_out, pend_out,
    pf, p_hi, p_lo, y_buf, y_cat, core_src, core_dst, part, first_dst, second_dst,
    rhs, inv_v, low_v, r0_all, y0_all, s1_all, r1,
    load_sem, own_sem, panel_sem, y_send, y_recv, core_send, core_recv, first_send, first_recv,
    second_send, second_recv, chain_send, chain_recv,
):
    steps, rows, depth = pf.shape
    wide = rhs.shape[2]
    chunks = core_send.shape[1]
    per = steps // chunks
    z = lax.axis_index("row")
    col = lax.axis_index("col")
    y, x, core = col // 4, (col // 2) % 2, col % 2
    chip = col // 2
    sibling = col + 1 - 2 * core
    x_near, y_near = col + 2 - 4 * x, col + 4 - 8 * y
    middle = (z == 1) | (z == 2)
    upper = z // 2
    z_fold = z + upper * (3 - 2 * z)

    def block_at(k):
        b = (z_fold, 1 - z_fold, 2, 3)[k]
        return b + upper * (3 - 2 * b)

    def half_of(h):
        return prior.at[:, h * wide:(h + 1) * wide]

    own = [pltpu.make_async_copy(half_of(h), y_buf.at[z, h], own_sem.at[h]) for h in range(2)]
    for copy in own:
        copy.start()

    def panel_copy(s):
        return pltpu.make_async_copy(panel.at[s], pf.at[s], panel_sem.at[s])

    for s in range(steps):
        panel_copy(s).start()
    loads = [
        pltpu.make_async_copy(right, rhs, load_sem.at[0]),
        pltpu.make_async_copy(inv, inv_v, load_sem.at[1]),
        pltpu.make_async_copy(lower, low_v, load_sem.at[2]),
    ]
    for copy in loads:
        copy.start()

    barrier = pltpu.get_barrier_semaphore()
    for partner in (sibling, x_near, y_near):
        pl.semaphore_signal(barrier, inc=1, device_id=(z, partner), device_id_type=MESH)
    for j in range(1, 4):
        pl.semaphore_signal(barrier, inc=1, device_id=((z + j) % 4, col), device_id_type=MESH)
    pl.semaphore_wait(barrier, 6)

    def along_z(src, b, h, target, sem):
        return pltpu.make_async_remote_copy(
            src_ref=src, dst_ref=y_buf.at[b, h], send_sem=y_send.at[sem, h],
            recv_sem=y_recv.at[b, h], device_id=(target, col), device_id_type=MESH,
        )

    def forward(b, h, finish=False):
        @pl.when((b < z) & (z < 3))
        def _():
            copy = along_z(y_buf.at[b, h], b, h, z + 1, 2 + b)
            copy.wait_send() if finish else copy.start()

        @pl.when((b > z) & (z > 0))
        def _():
            copy = along_z(y_buf.at[b, h], b, h, z - 1, 2 + b)
            copy.wait_send() if finish else copy.start()

    def own_sends(h, finish=False):
        @pl.when(z < 3)
        def _():
            copy = along_z(half_of(h), z, h, z + 1, 0)
            copy.wait_send() if finish else copy.start()

        @pl.when(z > 0)
        def _():
            copy = along_z(half_of(h), z, h, z - 1, 1)
            copy.wait_send() if finish else copy.start()

    def arrived(b, h):
        along_z(y_buf.at[b, h], b, h, (z + 1) % 4, 0).wait_recv()

    def piece(ref, k, c):
        return ref.at[k, pl.ds(c * per, per)]

    def order(c, along_x, along_y):
        return along_x + (c % 2) * (along_y - along_x)

    def core_copy(k, c):
        return pltpu.make_async_remote_copy(
            src_ref=piece(core_src, k, c), dst_ref=piece(core_dst, k, c),
            send_sem=core_send.at[k, c], recv_sem=core_recv.at[k, c],
            device_id=(z, sibling), device_id_type=MESH,
        )

    def first_copy(k, c):
        return pltpu.make_async_remote_copy(
            src_ref=piece(part, k, c), dst_ref=piece(first_dst, k, c),
            send_sem=first_send.at[k, c], recv_sem=first_recv.at[k, c],
            device_id=(z, order(c, x_near, y_near)), device_id_type=MESH,
        )

    def second_copy(k, c):
        return pltpu.make_async_remote_copy(
            src_ref=piece(part, k, c), dst_ref=second_dst.at[pl.ds(c * per, per)],
            send_sem=second_send.at[c], recv_sem=second_recv.at[c],
            device_id=(z, order(c, y_near, x_near)), device_id_type=MESH,
        )

    def first_away(k, c):
        b = block_at(k)
        return order(c, x, y) != order(c, b % 2, b // 2)

    def second_away(k, c):
        b = block_at(k)
        return order(c, y, x) != order(c, b // 2, b % 2)

    def multiply(k, h):
        high, low = split(y_buf[block_at(k), h])
        y_cat[:, :wide] = high
        y_cat[:, wide:] = low

        @pl.loop(0, chunks)
        def _(c):
            here = pl.ds(c * per, per)
            if k == 0 and h == 0:
                for i in range(per):
                    s = c * per + i
                    panel_copy(s).wait()
                    high, low = split(pf[s])
                    p_hi[s] = high
                    p_lo[s] = low
            left = p_hi[here].reshape(per * rows, depth)
            both = jnp.dot(left, y_cat[...], preferred_element_type=F32)
            left = p_lo[here].reshape(per * rows, depth)
            rest = jnp.dot(left, y_cat[:, :wide], preferred_element_type=F32)
            terms = (both[:, :wide] + (both[:, wide:] + rest)).reshape(per, rows, wide)

            @pl.when(core == h)
            def _():
                part[k, here] = terms

            @pl.when(core != h)
            def _():
                core_src[k, here] = terms
                core_copy(k, c).start()

    def add_core(k):
        @pl.loop(0, chunks)
        def _(c):
            core_copy(k, c).wait_recv()
            here = pl.ds(c * per, per)
            part[k, here] = part[k, here] + core_dst[k, here]

            @pl.when(first_away(k, c))
            def _():
                first_copy(k, c).start()

    def add_first(k, low, high):
        @pl.loop(low, high)
        def _(c):
            @pl.when(jnp.logical_not(first_away(k, c)))
            def _():
                first_copy(k, c).wait_recv()
                here = pl.ds(c * per, per)
                part[k, here] = part[k, here] + first_dst[k, here]

                @pl.when(second_away(k, c))
                def _():
                    second_copy(k, c).start()

    def chain_copy(which, ref, target, source):
        here = ref.at[pl.ds(pl.multiple_of(source * rows, rows), rows)]
        return pltpu.make_async_remote_copy(
            src_ref=here, dst_ref=here, send_sem=chain_send.at[which, target],
            recv_sem=chain_recv.at[which, source],
            device_id=(target, col), device_id_type=MESH,
        )

    def spread(which, ref, down, finish=False):
        for target in range(4):
            @pl.when((z != target) if down else (z < target))
            def _():
                copy = chain_copy(which, ref, target, z)
                copy.wait_send() if finish else copy.start()

    def collect(which, ref, down):
        for source in range(4):
            @pl.when((z != source) if down else (z > source))
            def _():
                chain_copy(which, ref, (z + 1) % 4, source).wait_recv()

    mine = pl.ds(pl.multiple_of(z * rows, rows), rows)

    def finish_block(k, low, high):
        @pl.when(block_at(k) == chip)
        def _():
            for c in range(low, high):
                second_copy(k, c).wait_recv()
                for s in range(c * per, (c + 1) * per):
                    rest = rhs[s] - (part[k, s] + second_dst[s])
                    if s == 0:
                        r0_all[mine, :] = rest
                        spread(0, r0_all, False)
                    elif s == 1:
                        r1[...] = rest
                    else:
                        pend_out[s - 2] = rest

    for h in range(2):
        own_sends(h)
    for ref in (r0_all, s1_all):
        for source in range(4):
            @pl.when(source > z)
            def _(ref=ref, source=source):
                ref[source * rows:(source + 1) * rows, :] = jnp.zeros((rows, wide), F32)

    for k in range(4):
        for h in range(2):
            if k == 0:
                own[h].wait()
            elif k == 2:
                @pl.when(jnp.logical_not(middle))
                def _():
                    arrived(block_at(2), h)
            else:
                arrived(block_at(k), h)
                forward(block_at(k), h)
            if k == 1:
                @pl.when(middle)
                def _():
                    arrived(block_at(2), h)
                    forward(block_at(2), h)
            multiply(k, h)
            if k == 0 and h == 0:
                for copy in loads:
                    copy.wait()

            @pl.when(core == h)
            def _():
                add_core(k)
                if k > 0:
                    finish_block(k - 1, 0, chunks)

            if h == 1 or k > 0:
                @pl.when(core != h)
                def _():
                    add_first(k if h == 1 else k - 1, 0, chunks)

    @pl.when(core == 1)
    def _():
        add_first(3, 0, 1)

    finish_block(3, 0, 1)

    @pl.when(core == 1)
    def _():
        add_first(3, 1, chunks)

    collect(0, r0_all, False)
    first_solution = dot3(split(inv_v[0]), split(r0_all[...]))
    y0_all[mine, :] = first_solution
    spread(1, y0_all, True)
    y_out[0] = first_solution
    finish_block(3, 1, chunks)
    collect(1, y0_all, True)
    s1_all[mine, :] = r1[...] - dot3(split(low_v[...]), split(y0_all[...]))
    spread(2, s1_all, False)
    collect(2, s1_all, False)
    y_out[1] = dot3(split(inv_v[1]), split(s1_all[...]))

    for h in range(2):
        own_sends(h, True)
        for k in range(1, 4):
            forward(block_at(k), h, True)
    for k in range(4):
        @pl.loop(0, chunks)
        def _(c):
            core_copy(k, c).wait_send()

            @pl.when(first_away(k, c))
            def _():
                first_copy(k, c).wait_send()

            @pl.when(jnp.logical_not(first_away(k, c)) & second_away(k, c))
            def _():
                second_copy(k, c).wait_send()

    spread(0, r0_all, False, True)
    spread(1, y0_all, True, True)
    spread(2, s1_all, False, True)


def fused(panel, prior_y, right_side, inv_blocks, lower_block):
    steps, rows, depth = panel.shape
    own = right_side.shape[2]
    size = inv_blocks.shape[2]
    chunks = 4
    anywhere = pl.BlockSpec(memory_space=pl.ANY)
    local = pl.BlockSpec(memory_space=pltpu.VMEM)
    dma = pltpu.SemaphoreType.DMA
    return pl.pallas_call(
        kernel,
        out_shape=(
            jax.ShapeDtypeStruct((2, rows, own), F32),
            jax.ShapeDtypeStruct((steps - 2, rows, own), F32),
        ),
        in_specs=[anywhere] * 5,
        out_specs=(local, local),
        scratch_shapes=[
            pltpu.VMEM((steps, rows, depth), F32),
            pltpu.VMEM((steps, rows, depth), BF16),
            pltpu.VMEM((steps, rows, depth), BF16),
            pltpu.VMEM((4, 2, depth, own), F32),
            pltpu.VMEM((depth, 2 * own), BF16),
            pltpu.VMEM((4, steps, rows, own), F32),
            pltpu.VMEM((4, steps, rows, own), F32),
            pltpu.VMEM((4, steps, rows, own), F32),
            pltpu.VMEM((4, steps, rows, own), F32),
            pltpu.VMEM((steps, rows, own), F32),
            pltpu.VMEM((steps, rows, own), F32),
            pltpu.VMEM((2, rows, size), F32),
            pltpu.VMEM((rows, size), F32),
            pltpu.VMEM((size, own), F32),
            pltpu.VMEM((size, own), F32),
            pltpu.VMEM((size, own), F32),
            pltpu.VMEM((rows, own), F32),
            dma((3,)),
            dma((2,)),
            dma((steps,)),
            dma((6, 2)),
            dma((4, 2)),
            dma((4, chunks)),
            dma((4, chunks)),
            dma((4, chunks)),
            dma((4, chunks)),
            dma((chunks,)),
            dma((chunks,)),
            dma((3, 4)),
            dma((3, 4)),
        ],
        compiler_params=pltpu.CompilerParams(
            collective_id=0, has_side_effects=True, vmem_limit_bytes=60 * 1024 * 1024
        ),
    )(panel, prior_y, right_side, inv_blocks, lower_block)


def general(panel, prior_y, right_side, inv_blocks, lower_block):
    highest = lax.Precision.HIGHEST
    terms = jnp.einsum(
        "sip,pm->sim",
        panel,
        lax.all_gather(prior_y, "row", axis=1, tiled=True),
        precision=highest,
        preferred_element_type=jnp.float32,
    )
    panel_total = lax.psum_scatter(terms, "col", scatter_dimension=2, tiled=True)
    residual = right_side - panel_total
    first_all_rows = lax.all_gather(residual[0], "row", axis=0, tiled=True)
    first_solution = jnp.dot(
        inv_blocks[0], first_all_rows, precision=highest, preferred_element_type=jnp.float32
    )
    solved_all = lax.all_gather(first_solution, "row", axis=0, tiled=True)
    second_residual = residual[1] - jnp.dot(
        lower_block, solved_all, precision=highest, preferred_element_type=jnp.float32
    )
    second_all_rows = lax.all_gather(second_residual, "row", axis=0, tiled=True)
    second_solution = jnp.dot(
        inv_blocks[1], second_all_rows, precision=highest, preferred_element_type=jnp.float32
    )
    return (jnp.stack([first_solution, second_solution]), residual[2:])


def solution(mesh):
    placed = (
        P(None, "row", "col"),
        P("col", "row"),
        P(None, "row", "col"),
        P(None, "row", None),
        P("row", None),
    )
    four_by_eight = mesh.shape["row"] == 4 and mesh.shape["col"] == 8
    return jax.shard_map(
        fused if four_by_eight else general,
        mesh=mesh,
        in_specs=placed,
        out_specs=(P(None, "row", "col"), P(None, "row", "col")),
        check_vma=False,
    )
```

```python
import functools

import jax
import jax.numpy as jnp
from jax import lax
from jax.experimental import pallas as pl
from jax.experimental.pallas import tpu as pltpu
from jax.sharding import PartitionSpec as P

MESH = pl.DeviceIdType.MESH
F32 = jnp.float32
BF16 = jnp.bfloat16


def split(x):
    high = x.astype(BF16)
    return high, (x - high.astype(F32)).astype(BF16)


def dot3(a, b):
    a_hi, a_lo = a
    b_hi, b_lo = b
    dot = functools.partial(jnp.dot, preferred_element_type=F32)
    return dot(a_hi, b_hi) + (dot(a_hi, b_lo) + dot(a_lo, b_hi))


def kernel(
    panel, prior, right, inv, lower, y_out, pend_out,
    pf, p_hi, p_lo, y_buf, y_cat, core_src, core_dst, part, first_dst, second_dst,
    rhs, inv_v, low_v, m_hi, m_lo, r0_all, y0_all, s1_all, r1,
    load_sem, own_sem, panel_sem, y_send, y_recv, core_send, core_recv, first_send, first_recv,
    second_send, second_recv, chain_send, chain_recv,
):
    steps, rows, depth = pf.shape
    wide = rhs.shape[2]
    chunks = core_send.shape[1]
    per = steps // chunks
    lag = 2
    z = lax.axis_index("row")
    col = lax.axis_index("col")
    y, x, core = col // 4, (col // 2) % 2, col % 2
    chip = col // 2
    sibling = col + 1 - 2 * core
    x_near, y_near = col + 2 - 4 * x, col + 4 - 8 * y
    middle = (z == 1) | (z == 2)
    upper = z // 2
    z_fold = z + upper * (3 - 2 * z)

    def block_at(k):
        b = (z_fold, 1 - z_fold, 2, 3)[k]
        return b + upper * (3 - 2 * b)

    def half_of(h):
        return prior.at[:, h * wide:(h + 1) * wide]

    own = [pltpu.make_async_copy(half_of(h), y_buf.at[z, h], own_sem.at[h]) for h in range(2)]
    for copy in own:
        copy.start()

    def panel_copy(s):
        return pltpu.make_async_copy(panel.at[s], pf.at[s], panel_sem.at[s])

    for s in range(steps):
        panel_copy(s).start()
    loads = [
        pltpu.make_async_copy(right, rhs, load_sem.at[0]),
        pltpu.make_async_copy(inv, inv_v, load_sem.at[1]),
        pltpu.make_async_copy(lower, low_v, load_sem.at[2]),
    ]
    for copy in loads:
        copy.start()

    barrier = pltpu.get_barrier_semaphore()
    for partner in (sibling, x_near, y_near):
        pl.semaphore_signal(barrier, inc=1, device_id=(z, partner), device_id_type=MESH)
    for j in range(1, 4):
        pl.semaphore_signal(barrier, inc=1, device_id=((z + j) % 4, col), device_id_type=MESH)
    pl.semaphore_wait(barrier, 6)

    def along_z(src, b, h, target, sem):
        return pltpu.make_async_remote_copy(
            src_ref=src, dst_ref=y_buf.at[b, h], send_sem=y_send.at[sem, h],
            recv_sem=y_recv.at[b, h], device_id=(target, col), device_id_type=MESH,
        )

    def forward(b, h, finish=False):
        @pl.when((b < z) & (z < 3))
        def _():
            copy = along_z(y_buf.at[b, h], b, h, z + 1, 2 + b)
            copy.wait_send() if finish else copy.start()

        @pl.when((b > z) & (z > 0))
        def _():
            copy = along_z(y_buf.at[b, h], b, h, z - 1, 2 + b)
            copy.wait_send() if finish else copy.start()

    def own_sends(h, finish=False):
        @pl.when(z < 3)
        def _():
            copy = along_z(half_of(h), z, h, z + 1, 0)
            copy.wait_send() if finish else copy.start()

        @pl.when(z > 0)
        def _():
            copy = along_z(half_of(h), z, h, z - 1, 1)
            copy.wait_send() if finish else copy.start()

    def arrived(b, h):
        along_z(y_buf.at[b, h], b, h, (z + 1) % 4, 0).wait_recv()

    def piece(ref, k, c):
        return ref.at[k, pl.ds(c * per, per)]

    def order(c, along_x, along_y):
        return along_x + (c % 2) * (along_y - along_x)

    def core_copy(k, c):
        return pltpu.make_async_remote_copy(
            src_ref=piece(core_src, k, c), dst_ref=piece(core_dst, k, c),
            send_sem=core_send.at[k, c], recv_sem=core_recv.at[k, c],
            device_id=(z, sibling), device_id_type=MESH,
        )

    def first_copy(k, c):
        return pltpu.make_async_remote_copy(
            src_ref=piece(part, k, c), dst_ref=piece(first_dst, k, c),
            send_sem=first_send.at[k, c], recv_sem=first_recv.at[k, c],
            device_id=(z, order(c, x_near, y_near)), device_id_type=MESH,
        )

    def second_copy(k, c):
        return pltpu.make_async_remote_copy(
            src_ref=piece(part, k, c), dst_ref=second_dst.at[pl.ds(c * per, per)],
            send_sem=second_send.at[c], recv_sem=second_recv.at[c],
            device_id=(z, order(c, y_near, x_near)), device_id_type=MESH,
        )

    def first_away(k, c):
        b = block_at(k)
        return order(c, x, y) != order(c, b % 2, b // 2)

    def second_away(k, c):
        b = block_at(k)
        return order(c, y, x) != order(c, b // 2, b % 2)

    def add_core(k, c):
        core_copy(k, c).wait_recv()
        here = pl.ds(c * per, per)
        part[k, here] = part[k, here] + core_dst[k, here]

        @pl.when(first_away(k, c))
        def _():
            first_copy(k, c).start()

    def multiply(k, h):
        high, low = split(y_buf[block_at(k), h])
        y_cat[:, :wide] = high
        y_cat[:, wide:] = low

        @pl.loop(0, chunks)
        def _(c):
            here = pl.ds(c * per, per)
            if k == 0 and h == 0:
                for i in range(per):
                    s = c * per + i
                    panel_copy(s).wait()
                    high, low = split(pf[s])
                    p_hi[s] = high
                    p_lo[s] = low
            left = p_hi[here].reshape(per * rows, depth)
            both = jnp.dot(left, y_cat[...], preferred_element_type=F32)
            left = p_lo[here].reshape(per * rows, depth)
            rest = jnp.dot(left, y_cat[:, :wide], preferred_element_type=F32)
            terms = (both[:, :wide] + (both[:, wide:] + rest)).reshape(per, rows, wide)

            @pl.when(core == h)
            def _():
                part[k, here] = terms

                @pl.when(c >= lag)
                def _():
                    add_core(k, c - lag)

            @pl.when(core != h)
            def _():
                core_src[k, here] = terms
                core_copy(k, c).start()

    def add_first(k, low, high):
        @pl.loop(low, high)
        def _(c):
            @pl.when(jnp.logical_not(first_away(k, c)))
            def _():
                first_copy(k, c).wait_recv()
                here = pl.ds(c * per, per)
                part[k, here] = part[k, here] + first_dst[k, here]

                @pl.when(second_away(k, c))
                def _():
                    second_copy(k, c).start()

    def chain_copy(which, ref, target, source):
        here = ref.at[pl.ds(pl.multiple_of(source * rows, rows), rows)]
        return pltpu.make_async_remote_copy(
            src_ref=here, dst_ref=here, send_sem=chain_send.at[which, target],
            recv_sem=chain_recv.at[which, source],
            device_id=(target, col), device_id_type=MESH,
        )

    def spread(which, ref, down, finish=False):
        for target in range(4):
            @pl.when((z != target) if down else (z < target))
            def _():
                copy = chain_copy(which, ref, target, z)
                copy.wait_send() if finish else copy.start()

    def collect(which, ref, down):
        for source in range(4):
            @pl.when((z != source) if down else (z > source))
            def _():
                chain_copy(which, ref, (z + 1) % 4, source).wait_recv()

    mine = pl.ds(pl.multiple_of(z * rows, rows), rows)

    def finish_block(k, low, high):
        @pl.when(block_at(k) == chip)
        def _():
            for c in range(low, high):
                second_copy(k, c).wait_recv()
                for s in range(c * per, (c + 1) * per):
                    rest = rhs[s] - (part[k, s] + second_dst[s])
                    if s == 0:
                        r0_all[mine, :] = rest
                        spread(0, r0_all, False)
                    elif s == 1:
                        r1[...] = rest
                    else:
                        pend_out[s - 2] = rest

    own_sends(0)
    own_sends(1)
    for ref in (r0_all, s1_all):
        for source in range(4):
            @pl.when(source > z)
            def _(ref=ref, source=source):
                ref[source * rows:(source + 1) * rows, :] = jnp.zeros((rows, wide), F32)

    for k in range(4):
        for h in range(2):
            if k == 0:
                own[h].wait()
            elif k == 2:
                @pl.when(jnp.logical_not(middle))
                def _():
                    arrived(block_at(2), h)
            else:
                arrived(block_at(k), h)
                forward(block_at(k), h)
            if k == 1:
                @pl.when(middle)
                def _():
                    arrived(block_at(2), h)
                    forward(block_at(2), h)
            multiply(k, h)
            if k == 0 and h == 0:
                for copy in loads:
                    copy.wait()
            if k == 0 and h == 1:
                for i, ref in enumerate((inv_v.at[0], low_v, inv_v.at[1])):
                    high, low = split(ref[...])
                    m_hi[i] = high
                    m_lo[i] = low

            @pl.when(core == h)
            def _():
                for c in range(chunks - lag, chunks):
                    add_core(k, c)
                if k > 0:
                    finish_block(k - 1, 0, chunks)

            if h == 1 or k > 0:
                @pl.when(core != h)
                def _():
                    add_first(k if h == 1 else k - 1, 0, chunks)

    @pl.when(core == 1)
    def _():
        add_first(3, 0, 1)

    finish_block(3, 0, 1)

    @pl.when(core == 1)
    def _():
        add_first(3, 1, chunks)

    collect(0, r0_all, False)
    first_solution = dot3((m_hi[0], m_lo[0]), split(r0_all[...]))
    y0_all[mine, :] = first_solution
    spread(1, y0_all, True)
    y_out[0] = first_solution
    finish_block(3, 1, chunks)
    collect(1, y0_all, True)
    s1_all[mine, :] = r1[...] - dot3((m_hi[1], m_lo[1]), split(y0_all[...]))
    spread(2, s1_all, False)
    collect(2, s1_all, False)
    y_out[1] = dot3((m_hi[2], m_lo[2]), split(s1_all[...]))

    for h in range(2):
        own_sends(h, True)
        for k in range(1, 4):
            forward(block_at(k), h, True)

    for k in range(4):
        @pl.loop(0, chunks)
        def _(c):
            core_copy(k, c).wait_send()

            @pl.when(first_away(k, c))
            def _():
                first_copy(k, c).wait_send()

            @pl.when(jnp.logical_not(first_away(k, c)) & second_away(k, c))
            def _():
                second_copy(k, c).wait_send()

    spread(0, r0_all, False, True)
    spread(1, y0_all, True, True)
    spread(2, s1_all, False, True)


def fused(panel, prior_y, right_side, inv_blocks, lower_block):
    steps, rows, depth = panel.shape
    own = right_side.shape[2]
    size = inv_blocks.shape[2]
    chunks = 8
    anywhere = pl.BlockSpec(memory_space=pl.ANY)
    local = pl.BlockSpec(memory_space=pltpu.VMEM)
    dma = pltpu.SemaphoreType.DMA
    return pl.pallas_call(
        kernel,
        out_shape=(
            jax.ShapeDtypeStruct((2, rows, own), F32),
            jax.ShapeDtypeStruct((steps - 2, rows, own), F32),
        ),
        in_specs=[anywhere] * 5,
        out_specs=(local, local),
        scratch_shapes=[
            pltpu.VMEM((steps, rows, depth), F32),
            pltpu.VMEM((steps, rows, depth), BF16),
            pltpu.VMEM((steps, rows, depth), BF16),
            pltpu.VMEM((4, 2, depth, own), F32),
            pltpu.VMEM((depth, 2 * own), BF16),
            pltpu.VMEM((4, steps, rows, own), F32),
            pltpu.VMEM((4, steps, rows, own), F32),
            pltpu.VMEM((4, steps, rows, own), F32),
            pltpu.VMEM((4, steps, rows, own), F32),
            pltpu.VMEM((steps, rows, own), F32),
            pltpu.VMEM((steps, rows, own), F32),
            pltpu.VMEM((2, rows, size), F32),
            pltpu.VMEM((rows, size), F32),
            pltpu.VMEM((3, rows, size), BF16),
            pltpu.VMEM((3, rows, size), BF16),
            pltpu.VMEM((size, own), F32),
            pltpu.VMEM((size, own), F32),
            pltpu.VMEM((size, own), F32),
            pltpu.VMEM((rows, own), F32),
            dma((3,)),
            dma((2,)),
            dma((steps,)),
            dma((6, 2)),
            dma((4, 2)),
            dma((4, chunks)),
            dma((4, chunks)),
            dma((4, chunks)),
            dma((4, chunks)),
            dma((chunks,)),
            dma((chunks,)),
            dma((3, 4)),
            dma((3, 4)),
        ],
        compiler_params=pltpu.CompilerParams(
            collective_id=0, has_side_effects=True, vmem_limit_bytes=60 * 1024 * 1024
        ),
    )(panel, prior_y, right_side, inv_blocks, lower_block)


def general(panel, prior_y, right_side, inv_blocks, lower_block):
    highest = lax.Precision.HIGHEST
    terms = jnp.einsum(
        "sip,pm->sim",
        panel,
        lax.all_gather(prior_y, "row", axis=1, tiled=True),
        precision=highest,
        preferred_element_type=jnp.float32,
    )
    panel_total = lax.psum_scatter(terms, "col", scatter_dimension=2, tiled=True)
    residual = right_side - panel_total
    first_all_rows = lax.all_gather(residual[0], "row", axis=0, tiled=True)
    first_solution = jnp.dot(
        inv_blocks[0], first_all_rows, precision=highest, preferred_element_type=jnp.float32
    )
    solved_all = lax.all_gather(first_solution, "row", axis=0, tiled=True)
    second_residual = residual[1] - jnp.dot(
        lower_block, solved_all, precision=highest, preferred_element_type=jnp.float32
    )
    second_all_rows = lax.all_gather(second_residual, "row", axis=0, tiled=True)
    second_solution = jnp.dot(
        inv_blocks[1], second_all_rows, precision=highest, preferred_element_type=jnp.float32
    )
    return (jnp.stack([first_solution, second_solution]), residual[2:])


def solution(mesh):
    placed = (
        P(None, "row", "col"),
        P("col", "row"),
        P(None, "row", "col"),
        P(None, "row", None),
        P("row", None),
    )
    four_by_eight = mesh.shape["row"] == 4 and mesh.shape["col"] == 8
    return jax.shard_map(
        fused if four_by_eight else general,
        mesh=mesh,
        in_specs=placed,
        out_specs=(P(None, "row", "col"), P(None, "row", "col")),
        check_vma=False,
    )
```
